32 devices in a mesh: seq: 16 (over z, y, x), head: 2 (over core).
Axes of the slice: x: 2, y: 2, z: 4, core: 2. Of those that a mesh axis runs over, the one named last changes fastest.
Arguments:
- queries: bfloat16 [4096, 4096], P('seq', 'head'), may hold values from -12 to 12
- key_input: bfloat16 [4096, 4096], P('seq', 'head'), may hold values from -1.796875 to 1.796875
- value_input: bfloat16 [4096, 4096], P('seq', 'head'), may hold values from -32 to 32
- norm_gain: bfloat16 [4096], P('head'), may hold values from 0.099609375 to 1.8984375
- out_weight: bfloat16 [4096, 3072], P('head', 'seq'), may hold values from -0.125 to 0.125
- target: bfloat16 [4096, 3072], P('seq', 'head'), may hold values from -6 to 6
Outputs:
- output: bfloat16 [4096, 3072], P('seq', 'head')
- query_grad: bfloat16 [4096, 4096], P('seq', 'head')
- key_grad: bfloat16 [4096, 4096], P('seq', 'head')
- value_grad: bfloat16 [4096, 4096], P('seq', 'head')
- gain_grads: float32 [16, 4096], P('seq', 'head')
- weight_grads: bfloat16 [16, 4096, 3072], P('seq', 'head')
The draws below stay inside these ranges and needn't reach their ends.
All inputs are finite; a program needn't handle non-finite values.
Results may differ from the reference program's by a relative error of at most 0.022.
Values may be sent and summed in bfloat16 or wider, within the bound.
A program may use at most 128 MiB of HBM per device.

```python
import math
import jax
import jax.numpy as jnp
from jax import lax

TOK_DEV = 256
HEADS = 32
HEAD_DIM = 128
OUT_WIDTH = 3072
FEATURES = 4096
TOKENS = 4096
N_SEQ = 16


def draw_queries(key, part):
    first, second = jax.random.split(jax.random.fold_in(key, 11))
    shape = (TOKENS, HEADS * HEAD_DIM)
    base = jnp.clip(jax.random.normal(first, shape, jnp.float32), -4.0, 4.0)
    spread = jnp.exp(jax.random.uniform(second, (TOKENS, 1), jnp.float32, 0.0, math.log(10.0)))
    return (0.3 * base * spread).astype(jnp.bfloat16)


def draw_value_input(key, part):
    first, second = jax.random.split(jax.random.fold_in(key, 23), 2)
    width = HEADS * HEAD_DIM
    shape = (TOKENS, width)
    ramp = jnp.arange(width, dtype=jnp.float32) / width
    jitter = jax.random.uniform(second, (1, width), jnp.float32, 0.0, math.log(10.0 / 3.0))
    base = jnp.clip(jax.random.normal(first, shape, jnp.float32), -3.0, 3.0)
    column = jnp.exp(math.log(3.0) * ramp[None, :] + jitter)
    return (0.2 * base * column).astype(jnp.bfloat16)


def raised(values, key, source, target, parts, factor):
    owner, partner = [(jnp.arange(values.shape[position]) // (values.shape[position] // parts)).reshape([-1 if axis == position else 1 for axis in range(values.ndim)]) for position in (source, target)]
    chosen = jax.random.permutation(key, parts)[partner]
    strong = (owner == chosen) | (owner == (partner + parts // 2) % parts)
    return jnp.where(strong, factor * values, values)


def block_scale(rng, shape, pieces, least, top_value):
    def one(axis_at, parts):
        steps = jax.random.uniform(jax.random.fold_in(jax.random.fold_in(rng, 6), axis_at), (parts,), jnp.float32, least / len(pieces), top_value / len(pieces))
        return jnp.repeat(jnp.exp(steps), shape[axis_at] // parts).reshape((-1,) + (1,) * (len(shape) - axis_at - 1))

    factor_of = one(*pieces[0])
    for cut in pieces[1:]:
        factor_of = factor_of * one(*cut)
    return factor_of


def gaussian(rng, dims, scale, most, pieces=(), held_as=jnp.bfloat16):
    gain = block_scale(rng, dims, pieces, -0.22, 0.18) if pieces else 1.0
    entries = jax.random.normal(rng, dims, jnp.float32) * scale * gain
    return jnp.minimum(jnp.maximum(entries, -most), most).astype(held_as)


def heavy_noise(rng, shape, scale, reach, cuts, heavy, held_as=jnp.bfloat16):
    array = scale * jax.random.normal(rng, shape, jnp.float32)
    if cuts:
        array = array * block_scale(rng, shape, cuts, -0.22, 0.18)
    return jnp.clip(raised(array, jax.random.fold_in(rng, 3), *heavy), -reach, reach).astype(held_as)


def setup_inputs(seed: int = 0) -> dict:
    key_of = jax.random.split(jax.random.key(seed), 7)
    queries = draw_queries(jax.random.fold_in(key_of[6], 71), 0)
    key_input = gaussian(key_of[1], (TOKENS, FEATURES), 0.3, 1.796875, ((0, 16), (1, 2)))
    value_input = draw_value_input(jax.random.fold_in(key_of[6], 71), 0)
    norm_gain = jnp.clip(1.0 + 0.18 * jax.random.normal(key_of[3], (FEATURES,), jnp.float32), 0.099609375, 1.8984375).astype(jnp.bfloat16)
    out_weight = heavy_noise(key_of[4], (FEATURES, OUT_WIDTH), FEATURES ** -0.5, 0.125, ((0, 2), (1, 16)), (0, 1, 16, 2.0))
    target = gaussian(key_of[5], (TOKENS, OUT_WIDTH), 1.0, 6.0, ((0, 16), (1, 2)))
    return {"queries": queries, "key_input": key_input, "value_input": value_input, "norm_gain": norm_gain, "out_weight": out_weight, "target": target}


EPSILON = 1e-06

def causal(count):
    row_index = lax.broadcasted_iota(jnp.int32, (count, count), 0)
    col_index = lax.broadcasted_iota(jnp.int32, (count, count), 1)
    return row_index >= col_index

def reference(queries, key_input, value_input, norm_gain, out_weight, target):
    shape4 = (N_SEQ, TOK_DEV, HEADS, HEAD_DIM)
    q_all = queries.reshape(shape4)
    k_all = key_input.reshape(shape4)
    v_all = value_input.reshape(shape4)
    keep_mask = causal(TOK_DEV)

    def forward_step(state, inputs):
        q_block, k_block, v_block = inputs
        q_float = q_block.astype(jnp.float32)
        k_float = k_block.astype(jnp.float32)
        v_float = v_block.astype(jnp.float32)
        state_low = state.astype(jnp.bfloat16)
        scores = jnp.einsum('thd,shd->hts', q_float, k_float)
        scores_low = jnp.where(keep_mask[None], scores, 0.0).astype(jnp.bfloat16)
        attended = jnp.einsum('hts,shd->thd', scores_low.astype(jnp.float32), v_float)
        attended = attended + jnp.einsum('thd,hde->the', q_float, state_low.astype(jnp.float32))
        state_next = state + jnp.einsum('shd,she->hde', k_float, v_float)
        return (state_next, (attended, state_low))
    zero_state = jnp.zeros((HEADS, HEAD_DIM, HEAD_DIM), jnp.float32)
    _, (attended, states) = lax.scan(forward_step, zero_state, (q_all, k_all, v_all))
    mixed = attended.reshape(TOKENS, FEATURES)
    gain_float = norm_gain.astype(jnp.float32)
    squares = lax.optimization_barrier(jnp.sum(mixed * mixed, axis=1, keepdims=True))
    inverse = lax.rsqrt(squares / FEATURES + EPSILON)
    normed = (mixed * inverse * gain_float).astype(jnp.bfloat16)
    projected = jnp.dot(normed, out_weight, preferred_element_type=jnp.float32)
    output = projected.astype(jnp.bfloat16)
    out_grad = (projected - target.astype(jnp.float32)).astype(jnp.bfloat16)
    normed_grad = jnp.dot(out_grad, out_weight.T, preferred_element_type=jnp.float32)
    inner = lax.optimization_barrier(jnp.sum(mixed * gain_float * normed_grad, axis=1, keepdims=True))
    mixed_grad = inverse * gain_float * normed_grad - mixed * inverse ** 3 * inner / FEATURES
    mixed_grad = mixed_grad.astype(jnp.bfloat16)
    gain_grads = lax.optimization_barrier(jnp.sum((normed_grad * mixed * inverse).reshape(N_SEQ, TOK_DEV, FEATURES), axis=1))

    def block_weight(pair):
        return lax.dot_general(pair[0], pair[1], (((0,), (0,)), ((), ())), preferred_element_type=jnp.float32).astype(jnp.bfloat16)
    weight_grads = lax.map(block_weight, (normed.reshape(N_SEQ, TOK_DEV, FEATURES), out_grad.reshape(N_SEQ, TOK_DEV, OUT_WIDTH)))
    grad_all = mixed_grad.reshape(shape4)

    def backward_step(later, inputs):
        q_block, k_block, v_block, grad_block, state_low = inputs
        q_float = q_block.astype(jnp.float32)
        k_float = k_block.astype(jnp.float32)
        v_float = v_block.astype(jnp.float32)
        grad_float = grad_block.astype(jnp.float32)
        state_float = state_low.astype(jnp.float32)
        later_float = later.astype(jnp.bfloat16).astype(jnp.float32)
        scores = jnp.einsum('thd,shd->hts', q_float, k_float)
        scores_float = jnp.where(keep_mask[None], scores, 0.0).astype(jnp.bfloat16).astype(jnp.float32)
        pairs = jnp.einsum('thd,shd->hts', grad_float, v_float)
        pairs_float = jnp.where(keep_mask[None], pairs, 0.0).astype(jnp.bfloat16).astype(jnp.float32)
        query_part = jnp.einsum('hts,shd->thd', pairs_float, k_float) + jnp.einsum('the,hde->thd', grad_float, state_float)
        key_part = jnp.einsum('hts,thd->shd', pairs_float, q_float) + jnp.einsum('she,hde->shd', v_float, later_float)
        value_part = jnp.einsum('hts,the->she', scores_float, grad_float) + jnp.einsum('shd,hde->she', k_float, later_float)
        later_next = later + jnp.einsum('thd,the->hde', q_float, grad_float)
        return (later_next, (query_part.astype(jnp.bfloat16), key_part.astype(jnp.bfloat16), value_part.astype(jnp.bfloat16)))
    _, (query_grad, key_grad, value_grad) = lax.scan(backward_step, zero_state, (q_all, k_all, v_all, grad_all, states), reverse=True)
    return (output, query_grad.reshape(TOKENS, FEATURES), key_grad.reshape(TOKENS, FEATURES), value_grad.reshape(TOKENS, FEATURES), gain_grads, weight_grads)
```

```python
import jax
import jax.numpy as jnp
from jax import lax
from jax.sharding import PartitionSpec as P

HEAD_DIM = 128
FEATURES = 4096


EPSILON = 1e-06


def entering(shard, axis, backward):
    count = lax.axis_size(axis)
    pieces = shard.astype(jnp.bfloat16).reshape(count, -1, shard.shape[-1])
    spread = lax.all_to_all(pieces, axis, 0, 0)
    row_index = lax.broadcasted_iota(jnp.int32, (count, count), 0)
    col_index = lax.broadcasted_iota(jnp.int32, (count, count), 1)
    chosen = col_index > row_index if backward else col_index < row_index
    sums = jnp.einsum(
        "ij,jrc->irc", chosen.astype(jnp.bfloat16), spread, preferred_element_type=jnp.float32
    )
    return lax.all_to_all(sums.astype(jnp.bfloat16), axis, 0, 0).reshape(shard.shape)


def causal(count):
    row_index = lax.broadcasted_iota(jnp.int32, (count, count), 0)
    col_index = lax.broadcasted_iota(jnp.int32, (count, count), 1)
    return row_index >= col_index


def per_device(queries, key_input, value_input, norm_gain, out_weight, target):
    tok_count = queries.shape[0]
    local_heads = queries.shape[1] // HEAD_DIM
    shape3 = (tok_count, local_heads, HEAD_DIM)
    q_heads = queries.reshape(shape3)
    k_heads = key_input.reshape(shape3)
    v_heads = value_input.reshape(shape3)
    keep_mask = causal(tok_count)
    f32 = jnp.float32
    state_local = jnp.einsum("shd,she->hde", k_heads, v_heads, preferred_element_type=f32)
    state_low = entering(state_local, "seq", False)
    scores = jnp.einsum("thd,shd->hts", q_heads, k_heads, preferred_element_type=f32)
    scores_low = jnp.where(keep_mask[None], scores, 0.0).astype(jnp.bfloat16)
    attended = jnp.einsum("hts,shd->thd", scores_low, v_heads, preferred_element_type=f32)
    attended = attended + jnp.einsum("thd,hde->the", q_heads, state_low, preferred_element_type=f32)
    mixed = attended.reshape(tok_count, -1)
    gain_float = norm_gain.astype(f32)
    squares = lax.psum(jnp.sum(mixed * mixed, axis=1, keepdims=True), "head")
    inverse = lax.rsqrt(squares / FEATURES + EPSILON)
    normed = (mixed * inverse * gain_float).astype(jnp.bfloat16)
    full_weight = lax.all_gather(out_weight, "seq", axis=1, tiled=True)
    partial_value = jnp.dot(normed, full_weight, preferred_element_type=f32)
    projected = lax.psum_scatter(
        partial_value.astype(jnp.bfloat16), "head", scatter_dimension=1, tiled=True
    ).astype(jnp.float32)
    output = projected.astype(jnp.bfloat16)
    grad_local = (projected - target.astype(f32)).astype(jnp.bfloat16)
    out_grad = lax.all_gather(grad_local, "head", axis=1, tiled=True)
    normed_grad = lax.dot_general(
        out_grad, full_weight, (((1,), (1,)), ((), ())), preferred_element_type=f32
    )
    product = jnp.sum(grad_local.astype(f32) * projected, axis=1, keepdims=True)
    inner = lax.psum(product, "head") / inverse
    mixed_grad = inverse * gain_float * normed_grad - mixed * inverse**3 * inner / FEATURES
    mixed_grad = mixed_grad.astype(jnp.bfloat16)
    gain_grads = jnp.sum(normed_grad * mixed * inverse, axis=0)[None]
    weight_grads = lax.dot_general(
        normed, out_grad, (((0,), (0,)), ((), ())), preferred_element_type=f32
    ).astype(jnp.bfloat16)[None]
    grad_heads = mixed_grad.reshape(shape3)
    grad_state = jnp.einsum("thd,the->hde", q_heads, grad_heads, preferred_element_type=f32)
    later_low = entering(grad_state, "seq", True)
    pairs = jnp.einsum("thd,shd->hts", grad_heads, v_heads, preferred_element_type=f32)
    pairs_low = jnp.where(keep_mask[None], pairs, 0.0).astype(jnp.bfloat16)
    query_grad = jnp.einsum("hts,shd->thd", pairs_low, k_heads, preferred_element_type=f32)
    query_grad = query_grad + jnp.einsum(
        "the,hde->thd", grad_heads, state_low, preferred_element_type=f32
    )
    key_grad = jnp.einsum("hts,thd->shd", pairs_low, q_heads, preferred_element_type=f32)
    key_grad = key_grad + jnp.einsum("she,hde->shd", v_heads, later_low, preferred_element_type=f32)
    value_grad = jnp.einsum("hts,the->she", scores_low, grad_heads, preferred_element_type=f32)
    value_grad = value_grad + jnp.einsum(
        "shd,hde->she", k_heads, later_low, preferred_element_type=f32
    )
    flat_shape = (tok_count, -1)
    return (
        output,
        query_grad.reshape(flat_shape).astype(jnp.bfloat16),
        key_grad.reshape(flat_shape).astype(jnp.bfloat16),
        value_grad.reshape(flat_shape).astype(jnp.bfloat16),
        gain_grads,
        weight_grads,
    )


def solution(mesh):
    placed = (
        P("seq", "head"),
        P("seq", "head"),
        P("seq", "head"),
        P("head"),
        P("head", "seq"),
        P("seq", "head"),
    )
    return jax.shard_map(
        per_device,
        mesh=mesh,
        in_specs=placed,
        out_specs=(
            P("seq", "head"),
            P("seq", "head"),
            P("seq", "head"),
            P("seq", "head"),
            P("seq", "head"),
            P("seq", "head", None),
        ),
        check_vma=False,
    )
```

```python
import functools

import jax
import jax.numpy as jnp
from jax import lax
from jax.experimental import pallas as pl
from jax.experimental.pallas import tpu as pltpu
from jax.sharding import PartitionSpec as P

HEAD_DIM = 128
FEATURES = 4096


EPSILON = 1e-06


def entering(shard, axis, backward):
    count = lax.axis_size(axis)
    pieces = shard.astype(jnp.bfloat16).reshape(count, -1, shard.shape[-1])
    spread = lax.all_to_all(pieces, axis, 0, 0)
    row_index = lax.broadcasted_iota(jnp.int32, (count, count), 0)
    col_index = lax.broadcasted_iota(jnp.int32, (count, count), 1)
    chosen = col_index > row_index if backward else col_index < row_index
    sums = jnp.einsum(
        "ij,jrc->irc", chosen.astype(jnp.bfloat16), spread, preferred_element_type=jnp.float32
    )
    return lax.all_to_all(sums.astype(jnp.bfloat16), axis, 0, 0).reshape(shard.shape)


def causal(count):
    row_index = lax.broadcasted_iota(jnp.int32, (count, count), 0)
    col_index = lax.broadcasted_iota(jnp.int32, (count, count), 1)
    return row_index >= col_index


def remote(src, dst, send_sem, recv_sem, peer):
    return pltpu.make_async_remote_copy(
        src_ref=src,
        dst_ref=dst,
        send_sem=send_sem,
        recv_sem=recv_sem,
        device_id={"seq": peer},
        device_id_type=pl.DeviceIdType.MESH,
    )


def exchange(count, me, source, target, send_sem, recv_sem):
    def start(step, carry):
        peer = lax.rem(me + step, count)
        remote(source.at[peer], target.at[me], send_sem.at[step], recv_sem.at[step], peer).start()
        return carry

    lax.fori_loop(1, count, start, 0)
    target[me] = source[me]


def exchange_wait(count, me, source, target, send_sem, recv_sem):
    def wait(step, carry):
        peer = lax.rem(me + step, count)
        origin = lax.rem(me - step + count, count)
        remote(source.at[peer], target.at[origin], send_sem.at[step], recv_sem.at[step], peer).wait()
        return carry

    lax.fori_loop(1, count, wait, 0)


def greet(count, me):
    barrier = pltpu.get_barrier_semaphore()

    def signal(step, carry):
        pl.semaphore_signal(
            barrier,
            inc=1,
            device_id={"seq": lax.rem(me + step, count)},
            device_id_type=pl.DeviceIdType.MESH,
        )
        return carry

    lax.fori_loop(1, count, signal, 0)
    pl.semaphore_wait(barrier, count - 1)


def running_sums(count, source, target, backward):
    def one(step, total):
        index = count - 1 - step if backward else step
        target[index] = total.astype(jnp.bfloat16)
        return total + source[index].astype(jnp.float32)

    lax.fori_loop(0, count, one, jnp.zeros(source.shape[1:], jnp.float32))


def columns_of(head):
    return pl.ds(pl.multiple_of(head * HEAD_DIM, HEAD_DIM), HEAD_DIM)


def pieces_of(head, per_head):
    return pl.ds(head * per_head, per_head)


def dims(left, right):
    return (((left,), (right,)), ((), ()))


def forward_kernel(
    count,
    q_ref,
    k_ref,
    v_ref,
    w_ref,
    full_ref,
    mixed_ref,
    scores_ref,
    state_ref,
    mine_ref,
    spread_ref,
    sums_ref,
    x_sem,
    y_sem,
    up_sem,
    down_sem,
    land_sem,
    first_send,
    first_recv,
    second_send,
    second_recv,
    own_sem,
):
    f32 = jnp.float32
    me = lax.axis_index("seq")
    layers = count // 4
    layer, plane = me // 4, lax.rem(me, 4)
    row, col = plane // 2, lax.rem(plane, 2)
    plane_x = row * 2 + (1 - col)
    plane_y = (1 - row) * 2 + col
    plane_d = (1 - row) * 2 + (1 - col)
    x_peer = layer * 4 + plane_x
    y_peer = layer * 4 + plane_y
    features = w_ref.shape[1]
    blocks = features // 128
    cut_a = blocks // 4
    cut_b = cut_a + (blocks - cut_a + 1) // 2
    edges = (0, cut_a * 128, cut_b * 128, features)
    piece = [pl.ds(edges[i], edges[i + 1] - edges[i]) for i in range(3)]
    local_heads = features // HEAD_DIM
    per_head = HEAD_DIM // mine_ref.shape[1]
    tok_count = q_ref.shape[0]

    def copy(shard, part, send_sem, peer, own=False):
        src = w_ref.at[:, piece[part]] if own else full_ref.at[shard, :, piece[part]]
        return remote(
            src, full_ref.at[shard, :, piece[part]], send_sem, land_sem.at[shard, part], peer
        )

    def landed(shard, part):
        copy(shard, part, x_sem.at[layers, 2], x_peer).wait_recv()

    def to_x(at, slot, shard, part, own=False):
        return copy(shard, part, x_sem.at[at, slot], x_peer, own)

    def to_y(at, slot, shard, part, own=False):
        return copy(shard, part, y_sem.at[at, slot], y_peer, own)

    def vertical(up, at, slot, shard, part, act, own=False, slack=None):
        sem, peer = (up_sem, me + 4) if up else (down_sem, me - 4)
        room = layers - 2 - layer if up else layer - 1
        room = room if slack is None else jnp.minimum(room, slack)

        @pl.when(room >= 0)
        def _():
            act(copy(shard, part, sem.at[at, slot], peer, own))

    def begin(transfer):
        transfer.start()

    def finish(transfer):
        transfer.wait_send()

    def own_sends(act):
        for part in (1, 2):
            for up in (True, False):
                vertical(up, layer, part - 1, me, part, act, True)
            act(to_x(layer, part - 1, me, part, True))
            act(to_y(layer, part - 1, me, part, True))
        act(to_x(layers, 0, me, 0, True))
        act(to_y(layers, 0, me, 0, True))
        for up in (True, False):
            vertical(up, layer, 2 + 0, me, 0, act, True)

    def sources(step):
        if step == 0:
            return ((layer, None, None),)
        return (
            (layer - step, layer - step, True),
            (layer + step, layers - 1 - layer - step, False),
        )

    def column_step(step, act, waiting):
        for at, slack, up in sources(step):
            shard = at * 4 + plane
            for part in (1, 2):

                @pl.when(slack >= 0)
                def _():
                    if waiting:
                        landed(shard, part)
                    act(to_x(at, part - 1, shard, part))
                    act(to_y(at, part - 1, shard, part))

                vertical(up, at, part - 1, shard, part, act, slack=slack)

    def guarded(slack, body):
        if slack is None:
            body()
        else:
            pl.when(slack >= 0)(body)

    def diagonal_step(step, act, waiting):
        for at, slack, _unused in sources(step):

            def body(at=at):
                if waiting:
                    landed(at * 4 + plane_y, 1)
                act(to_x(at, 2, at * 4 + plane_y, 1))
                if waiting:
                    landed(at * 4 + plane_x, 2)
                act(to_y(at, 2, at * 4 + plane_x, 2))

            guarded(slack, body)

    others = (plane_x, plane_y, plane_d)

    def plane_step(act, waiting):
        for slot, other in enumerate(others):
            shard = layer * 4 + other
            if waiting:
                landed(shard, 0)
            if slot == 0:
                act(to_y(layers, 1, shard, 0))
            for up in (True, False):
                vertical(up, layer, 3 + slot, shard, 0, act)

    def plane_chain(step, act, waiting):
        for at, slack, up in sources(step):
            for slot, other in enumerate((plane,) + others):
                shard = at * 4 + other
                if waiting:

                    @pl.when(slack >= 0)
                    def _():
                        landed(shard, 0)

                vertical(up, at, 2 + slot, shard, 0, act, slack=slack)

    greet(count, me)
    own_sends(begin)
    own = pltpu.make_async_copy(w_ref, full_ref.at[me], own_sem)
    own.start()

    def outer(head, carry):
        cols = columns_of(head)
        state = lax.dot_general(
            k_ref[:, cols], v_ref[:, cols], dims(0, 0), preferred_element_type=f32
        )
        state = state.reshape((per_head,) + mine_ref.shape[1:])
        mine_ref[pieces_of(head, per_head)] = state.astype(jnp.bfloat16)
        return carry

    lax.fori_loop(0, local_heads, outer, 0)
    exchange(count, me, mine_ref, spread_ref, first_send, first_recv)
    keep = causal(tok_count)

    def inside(head, carry):
        cols = columns_of(head)
        scores = lax.dot_general(
            q_ref[:, cols], k_ref[:, cols], dims(1, 1), preferred_element_type=f32
        )
        scores = jnp.where(keep, scores, 0.0).astype(jnp.bfloat16)
        scores_ref[head] = scores
        mixed_ref[:, cols] = jnp.dot(scores, v_ref[:, cols], preferred_element_type=f32)
        return carry

    lax.fori_loop(0, local_heads, inside, 0)
    column_step(1, begin, True)
    diagonal_step(0, begin, True)
    plane_step(begin, True)
    exchange_wait(count, me, mine_ref, spread_ref, first_send, first_recv)
    running_sums(count, spread_ref, sums_ref, False)
    exchange(count, me, sums_ref, state_ref, second_send, second_recv)
    for step in range(2, layers):
        column_step(step, begin, True)
        diagonal_step(step - 1, begin, True)
        plane_chain(step - 1, begin, True)
    exchange_wait(count, me, sums_ref, state_ref, second_send, second_recv)

    def across(head, carry):
        cols = columns_of(head)
        state = state_ref[pieces_of(head, per_head)].reshape(HEAD_DIM, HEAD_DIM)
        mixed_ref[:, cols] += jnp.dot(q_ref[:, cols], state, preferred_element_type=f32)
        return carry

    lax.fori_loop(0, local_heads, across, 0)
    diagonal_step(layers - 1, begin, True)
    plane_chain(layers - 1, begin, True)
    for at in range(layers):
        landed(at * 4 + plane_x, 1)
        landed(at * 4 + plane_y, 2)
        landed(at * 4 + plane_d, 1)
        landed(at * 4 + plane_d, 2)
    own_sends(finish)
    plane_step(finish, False)
    diagonal_step(0, finish, False)
    for step in range(1, layers):
        column_step(step, finish, False)
        diagonal_step(step, finish, False)
        plane_chain(step, finish, False)
    own.wait()


def forward_part(queries, key_input, value_input, weight):
    count = lax.axis_size("seq")
    tok_count, features = queries.shape
    local_heads = features // HEAD_DIM
    layers = count // 4
    piece_shape = (count, local_heads * HEAD_DIM // count, HEAD_DIM)
    low = jnp.bfloat16
    vmem = pl.BlockSpec(memory_space=pltpu.VMEM)
    dma = pltpu.SemaphoreType.DMA
    return pl.pallas_call(
        functools.partial(forward_kernel, count),
        out_shape=(
            jax.ShapeDtypeStruct((count,) + weight.shape, low),
            jax.ShapeDtypeStruct((tok_count, features), jnp.float32),
            jax.ShapeDtypeStruct((local_heads, tok_count, tok_count), low),
            jax.ShapeDtypeStruct(piece_shape, low),
        ),
        in_specs=[vmem] * 4,
        out_specs=(pl.BlockSpec(memory_space=pl.ANY), vmem, vmem, vmem),
        scratch_shapes=[
            pltpu.VMEM(piece_shape, low),
            pltpu.VMEM(piece_shape, low),
            pltpu.VMEM(piece_shape, low),
            dma((layers + 1, 3)),
            dma((layers + 1, 3)),
            dma((layers, 6)),
            dma((layers, 6)),
            dma((count, 3)),
            dma((count,)),
            dma((count,)),
            dma((count,)),
            dma((count,)),
            dma(()),
        ],
        compiler_params=pltpu.CompilerParams(collective_id=0, has_side_effects=True),
        name="forward_part",
    )(queries, key_input, value_input, weight)


def per_device(queries, key_input, value_input, norm_gain, out_weight, target):
    tok_count = queries.shape[0]
    local_heads = queries.shape[1] // HEAD_DIM
    shape3 = (tok_count, local_heads, HEAD_DIM)
    q_heads = queries.reshape(shape3)
    k_heads = key_input.reshape(shape3)
    v_heads = value_input.reshape(shape3)
    keep_mask = causal(tok_count)
    f32 = jnp.float32
    gathered, mixed, scores_low, state_low = forward_part(
        queries, key_input, value_input, out_weight.T
    )
    state_low = state_low.reshape(local_heads, HEAD_DIM, HEAD_DIM)
    full_weight = gathered.reshape(-1, gathered.shape[2])
    gain_float = norm_gain.astype(f32)
    squares = lax.psum(jnp.sum(mixed * mixed, axis=1, keepdims=True), "head")
    inverse = lax.rsqrt(squares / FEATURES + EPSILON)
    normed = (mixed * inverse * gain_float).astype(jnp.bfloat16)
    partial_value = lax.dot_general(
        normed, full_weight, (((1,), (1,)), ((), ())), preferred_element_type=f32
    )
    projected = lax.psum_scatter(
        partial_value.astype(jnp.bfloat16), "head", scatter_dimension=1, tiled=True
    ).astype(jnp.float32)
    output = projected.astype(jnp.bfloat16)
    grad_local = (projected - target.astype(f32)).astype(jnp.bfloat16)
    out_grad = lax.all_gather(grad_local, "head", axis=1, tiled=True)
    normed_grad = lax.dot_general(
        out_grad, full_weight, (((1,), (0,)), ((), ())), preferred_element_type=f32
    )
    product = jnp.sum(grad_local.astype(f32) * projected, axis=1, keepdims=True)
    inner = lax.psum(product, "head") / inverse
    mixed_grad = inverse * gain_float * normed_grad - mixed * inverse**3 * inner / FEATURES
    mixed_grad = mixed_grad.astype(jnp.bfloat16)
    gain_grads = jnp.sum(normed_grad * mixed * inverse, axis=0)[None]
    weight_grads = lax.dot_general(
        normed, out_grad, (((0,), (0,)), ((), ())), preferred_element_type=f32
    ).astype(jnp.bfloat16)[None]
    grad_heads = mixed_grad.reshape(shape3)
    grad_state = jnp.einsum("thd,the->hde", q_heads, grad_heads, preferred_element_type=f32)
    later_low = entering(grad_state, "seq", True)
    pairs = jnp.einsum("thd,shd->hts", grad_heads, v_heads, preferred_element_type=f32)
    pairs_low = jnp.where(keep_mask[None], pairs, 0.0).astype(jnp.bfloat16)
    query_grad = jnp.einsum("hts,shd->thd", pairs_low, k_heads, preferred_element_type=f32)
    query_grad = query_grad + jnp.einsum(
        "the,hde->thd", grad_heads, state_low, preferred_element_type=f32
    )
    key_grad = jnp.einsum("hts,thd->shd", pairs_low, q_heads, preferred_element_type=f32)
    key_grad = key_grad + jnp.einsum("she,hde->shd", v_heads, later_low, preferred_element_type=f32)
    value_grad = jnp.einsum("hts,the->she", scores_low, grad_heads, preferred_element_type=f32)
    value_grad = value_grad + jnp.einsum(
        "shd,hde->she", k_heads, later_low, preferred_element_type=f32
    )
    flat_shape = (tok_count, -1)
    return (
        output,
        query_grad.reshape(flat_shape).astype(jnp.bfloat16),
        key_grad.reshape(flat_shape).astype(jnp.bfloat16),
        value_grad.reshape(flat_shape).astype(jnp.bfloat16),
        gain_grads,
        weight_grads,
    )


def solution(mesh):
    placed = (
        P("seq", "head"),
        P("seq", "head"),
        P("seq", "head"),
        P("head"),
        P("head", "seq"),
        P("seq", "head"),
    )
    return jax.shard_map(
        per_device,
        mesh=mesh,
        in_specs=placed,
        out_specs=(
            P("seq", "head"),
            P("seq", "head"),
            P("seq", "head"),
            P("seq", "head"),
            P("seq", "head"),
            P("seq", "head", None),
        ),
        check_vma=False,
    )
```

```python
import functools

import jax
import jax.numpy as jnp
from jax import lax
from jax.experimental import pallas as pl
from jax.experimental.pallas import tpu as pltpu
from jax.sharding import PartitionSpec as P

HEAD_DIM = 128
FEATURES = 4096


EPSILON = 1e-06


def causal(count):
    row_index = lax.broadcasted_iota(jnp.int32, (count, count), 0)
    col_index = lax.broadcasted_iota(jnp.int32, (count, count), 1)
    return row_index >= col_index


def remote(src, dst, send_sem, recv_sem, peer, axis="seq"):
    return pltpu.make_async_remote_copy(
        src_ref=src,
        dst_ref=dst,
        send_sem=send_sem,
        recv_sem=recv_sem,
        device_id={axis: peer},
        device_id_type=pl.DeviceIdType.MESH,
    )


def exchange(count, me, source, target, send_sem, recv_sem):
    def start(step, carry):
        peer = lax.rem(me + step, count)
        remote(source.at[peer], target.at[me], send_sem.at[step], recv_sem.at[step], peer).start()
        return carry

    lax.fori_loop(1, count, start, 0)
    target[me] = source[me]


def exchange_wait(count, me, source, target, send_sem, recv_sem):
    def wait(step, carry):
        peer = lax.rem(me + step, count)
        origin = lax.rem(me - step + count, count)
        remote(source.at[peer], target.at[origin], send_sem.at[step], recv_sem.at[step], peer).wait()
        return carry

    lax.fori_loop(1, count, wait, 0)


def greet(*axes):
    barrier = pltpu.get_barrier_semaphore()
    for axis, count, me in axes:

        def signal(step, carry):
            pl.semaphore_signal(
                barrier,
                inc=1,
                device_id={axis: lax.rem(me + step, count)},
                device_id_type=pl.DeviceIdType.MESH,
            )
            return carry

        lax.fori_loop(1, count, signal, 0)
    pl.semaphore_wait(barrier, sum(count - 1 for _unused, count, _unused2 in axes))


def running_sums(count, source, target, backward):
    def one(step, total):
        index = count - 1 - step if backward else step
        target[index] = total.astype(jnp.bfloat16)
        return total + source[index].astype(jnp.float32)

    lax.fori_loop(0, count, one, jnp.zeros(source.shape[1:], jnp.float32))


def columns_of(head):
    return pl.ds(pl.multiple_of(head * HEAD_DIM, HEAD_DIM), HEAD_DIM)


def pieces_of(head, per_head):
    return pl.ds(head * per_head, per_head)


def dims(left, right):
    return (((left,), (right,)), ((), ()))


def forward_kernel(
    count,
    q_ref,
    k_ref,
    v_ref,
    w_ref,
    full_ref,
    mixed_ref,
    scores_ref,
    state_ref,
    mine_ref,
    spread_ref,
    sums_ref,
    x_sem,
    y_sem,
    up_sem,
    down_sem,
    land_sem,
    first_send,
    first_recv,
    second_send,
    second_recv,
    own_sem,
):
    f32 = jnp.float32
    me = lax.axis_index("seq")
    layers = count // 4
    layer, plane = me // 4, lax.rem(me, 4)
    row, col = plane // 2, lax.rem(plane, 2)
    plane_x = row * 2 + (1 - col)
    plane_y = (1 - row) * 2 + col
    plane_d = (1 - row) * 2 + (1 - col)
    x_peer = layer * 4 + plane_x
    y_peer = layer * 4 + plane_y
    features = w_ref.shape[1]
    blocks = features // 128
    cut_a = blocks // 4
    cut_b = cut_a + (blocks - cut_a + 1) // 2
    edges = (0, cut_a * 128, cut_b * 128, features)
    piece = [pl.ds(edges[i], edges[i + 1] - edges[i]) for i in range(3)]
    local_heads = features // HEAD_DIM
    per_head = HEAD_DIM // mine_ref.shape[1]
    tok_count = q_ref.shape[0]

    def copy(shard, part, send_sem, peer, own=False):
        src = w_ref.at[:, piece[part]] if own else full_ref.at[shard, :, piece[part]]
        return remote(
            src, full_ref.at[shard, :, piece[part]], send_sem, land_sem.at[shard, part], peer
        )

    def landed(shard, part):
        copy(shard, part, x_sem.at[layers, 2], x_peer).wait_recv()

    def to_x(at, slot, shard, part, own=False):
        return copy(shard, part, x_sem.at[at, slot], x_peer, own)

    def to_y(at, slot, shard, part, own=False):
        return copy(shard, part, y_sem.at[at, slot], y_peer, own)

    def vertical(up, at, slot, shard, part, act, own=False, slack=None):
        sem, peer = (up_sem, me + 4) if up else (down_sem, me - 4)
        room = layers - 2 - layer if up else layer - 1
        room = room if slack is None else jnp.minimum(room, slack)

        @pl.when(room >= 0)
        def _():
            act(copy(shard, part, sem.at[at, slot], peer, own))

    def begin(transfer):
        transfer.start()

    def finish(transfer):
        transfer.wait_send()

    def own_sends(act):
        for part in (1, 2):
            for up in (True, False):
                vertical(up, layer, part - 1, me, part, act, True)
            act(to_x(layer, part - 1, me, part, True))
            act(to_y(layer, part - 1, me, part, True))
        act(to_x(layers, 0, me, 0, True))
        act(to_y(layers, 0, me, 0, True))
        for up in (True, False):
            vertical(up, layer, 2 + 0, me, 0, act, True)

    def sources(step):
        if step == 0:
            return ((layer, None, None),)
        return (
            (layer - step, layer - step, True),
            (layer + step, layers - 1 - layer - step, False),
        )

    def column_step(step, act, waiting):
        for at, slack, up in sources(step):
            shard = at * 4 + plane
            for part in (1, 2):

                @pl.when(slack >= 0)
                def _():
                    if waiting:
                        landed(shard, part)
                    act(to_x(at, part - 1, shard, part))
                    act(to_y(at, part - 1, shard, part))

                vertical(up, at, part - 1, shard, part, act, slack=slack)

    def guarded(slack, body):
        if slack is None:
            body()
        else:
            pl.when(slack >= 0)(body)

    def diagonal_step(step, act, waiting):
        for at, slack, _unused in sources(step):

            def body(at=at):
                if waiting:
                    landed(at * 4 + plane_y, 1)
                act(to_x(at, 2, at * 4 + plane_y, 1))
                if waiting:
                    landed(at * 4 + plane_x, 2)
                act(to_y(at, 2, at * 4 + plane_x, 2))

            guarded(slack, body)

    others = (plane_x, plane_y, plane_d)

    def plane_step(act, waiting):
        for slot, other in enumerate(others):
            shard = layer * 4 + other
            if waiting:
                landed(shard, 0)
            if slot == 0:
                act(to_y(layers, 1, shard, 0))
            for up in (True, False):
                vertical(up, layer, 3 + slot, shard, 0, act)

    def plane_chain(step, act, waiting):
        for at, slack, up in sources(step):
            for slot, other in enumerate((plane,) + others):
                shard = at * 4 + other
                if waiting:

                    @pl.when(slack >= 0)
                    def _():
                        landed(shard, 0)

                vertical(up, at, 2 + slot, shard, 0, act, slack=slack)

    greet(("seq", count, me))
    own_sends(begin)
    own = pltpu.make_async_copy(w_ref, full_ref.at[me], own_sem)
    own.start()

    def outer(head, carry):
        cols = columns_of(head)
        state = lax.dot_general(
            k_ref[:, cols], v_ref[:, cols], dims(0, 0), preferred_element_type=f32
        )
        state = state.reshape((per_head,) + mine_ref.shape[1:])
        mine_ref[pieces_of(head, per_head)] = state.astype(jnp.bfloat16)
        return carry

    lax.fori_loop(0, local_heads, outer, 0)
    exchange(count, me, mine_ref, spread_ref, first_send, first_recv)
    keep = causal(tok_count)

    def inside(head, carry):
        cols = columns_of(head)
        scores = lax.dot_general(
            q_ref[:, cols], k_ref[:, cols], dims(1, 1), preferred_element_type=f32
        )
        scores = jnp.where(keep, scores, 0.0).astype(jnp.bfloat16)
        scores_ref[head] = scores
        mixed_ref[:, cols] = jnp.dot(scores, v_ref[:, cols], preferred_element_type=f32)
        return carry

    lax.fori_loop(0, local_heads, inside, 0)
    column_step(1, begin, True)
    diagonal_step(0, begin, True)
    plane_step(begin, True)
    exchange_wait(count, me, mine_ref, spread_ref, first_send, first_recv)
    running_sums(count, spread_ref, sums_ref, False)
    exchange(count, me, sums_ref, state_ref, second_send, second_recv)
    for step in range(2, layers):
        column_step(step, begin, True)
        diagonal_step(step - 1, begin, True)
        plane_chain(step - 1, begin, True)
    exchange_wait(count, me, sums_ref, state_ref, second_send, second_recv)

    def across(head, carry):
        cols = columns_of(head)
        state = state_ref[pieces_of(head, per_head)].reshape(HEAD_DIM, HEAD_DIM)
        mixed_ref[:, cols] += jnp.dot(q_ref[:, cols], state, preferred_element_type=f32)
        return carry

    lax.fori_loop(0, local_heads, across, 0)
    diagonal_step(layers - 1, begin, True)
    plane_chain(layers - 1, begin, True)
    for at in range(layers):
        landed(at * 4 + plane_x, 1)
        landed(at * 4 + plane_y, 2)
        landed(at * 4 + plane_d, 1)
        landed(at * 4 + plane_d, 2)
    own_sends(finish)
    plane_step(finish, False)
    diagonal_step(0, finish, False)
    for step in range(1, layers):
        column_step(step, finish, False)
        diagonal_step(step, finish, False)
        plane_chain(step, finish, False)
    own.wait()


def forward_part(queries, key_input, value_input, weight):
    count = lax.axis_size("seq")
    tok_count, features = queries.shape
    local_heads = features // HEAD_DIM
    layers = count // 4
    piece_shape = (count, local_heads * HEAD_DIM // count, HEAD_DIM)
    low = jnp.bfloat16
    vmem = pl.BlockSpec(memory_space=pltpu.VMEM)
    dma = pltpu.SemaphoreType.DMA
    return pl.pallas_call(
        functools.partial(forward_kernel, count),
        out_shape=(
            jax.ShapeDtypeStruct((count,) + weight.shape, low),
            jax.ShapeDtypeStruct((tok_count, features), jnp.float32),
            jax.ShapeDtypeStruct((local_heads, tok_count, tok_count), low),
            jax.ShapeDtypeStruct(piece_shape, low),
        ),
        in_specs=[vmem] * 4,
        out_specs=(pl.BlockSpec(memory_space=pl.ANY), vmem, vmem, vmem),
        scratch_shapes=[
            pltpu.VMEM(piece_shape, low),
            pltpu.VMEM(piece_shape, low),
            pltpu.VMEM(piece_shape, low),
            dma((layers + 1, 3)),
            dma((layers + 1, 3)),
            dma((layers, 6)),
            dma((layers, 6)),
            dma((count, 3)),
            dma((count,)),
            dma((count,)),
            dma((count,)),
            dma((count,)),
            dma(()),
        ],
        compiler_params=pltpu.CompilerParams(collective_id=0, has_side_effects=True),
        name="forward_part",
    )(queries, key_input, value_input, weight)


def backward_kernel(
    count,
    groups,
    mixed_ref,
    gain_ref,
    w_hbm,
    target_ref,
    q_ref,
    k_ref,
    v_ref,
    scores_ref,
    state_ref,
    output_ref,
    normed_ref,
    out_grad_ref,
    query_ref,
    key_ref,
    value_ref,
    gain_grad_ref,
    w_ref,
    part_mine,
    part_land,
    own_part,
    square_mine,
    square_land,
    product_mine,
    product_land,
    normed_grad_ref,
    key_part,
    mixed_grad_ref,
    mine_ref,
    spread_ref,
    sums_ref,
    later_ref,
    w_sem,
    head_send,
    head_recv,
    first_send,
    first_recv,
    second_send,
    second_recv,
):
    f32 = jnp.float32
    low = jnp.bfloat16
    me = lax.axis_index("seq")
    group = lax.axis_index("head")
    tok_count, features = q_ref.shape
    block = target_ref.shape[1]
    tile = 256 if block % 256 == 0 else 128
    wide = 256
    local_heads = features // HEAD_DIM
    per_head = HEAD_DIM // mine_ref.shape[1]
    ahead = [lax.rem(group + step, groups) for step in range(groups)]
    behind = [lax.rem(group + groups - step, groups) for step in range(groups)]

    def block_rows(index):
        return pl.ds(pl.multiple_of(index * block, block), block)

    def tile_of(index, size, base=0):
        return pl.ds(pl.multiple_of(base + index * size, size), size)

    def w_copy(step):
        rows = block_rows(ahead[step])
        return pltpu.make_async_copy(w_hbm.at[rows], w_ref.at[rows], w_sem.at[step])

    def head_copy(kind, step, src, dst):
        return remote(
            src, dst, head_send.at[kind, step], head_recv.at[kind, step], ahead[step], "head"
        )

    def square_copy(step):
        return head_copy(0, step, square_mine, square_land.at[step])

    def part_copy(step):
        return head_copy(1, step, part_mine.at[step], part_land.at[step])

    def product_copy(step):
        return head_copy(2, step, product_mine, product_land.at[step])

    def grad_copy(step, index):
        cols = block_rows(index)
        return head_copy(3, step, out_grad_ref.at[:, cols], out_grad_ref.at[:, cols])

    order = list(range(1, groups)) + [0]
    for step in order:
        w_copy(step).start()
    greet(("seq", count, me), ("head", groups, group))

    def squared(index, total):
        value = mixed_ref[:, tile_of(index, wide)]
        return total + jnp.sum(value * value, axis=1, keepdims=True)

    squares = lax.fori_loop(0, features // wide, squared, jnp.zeros((tok_count, 1), f32))
    square_mine[...] = jnp.broadcast_to(squares, square_mine.shape)
    for step in range(1, groups):
        square_copy(step).start()
    for step in range(1, groups):
        square_copy(step).wait()
        squares = squares + square_land[step][:, :1]
    inverse = lax.rsqrt(squares / FEATURES + EPSILON)

    def normalize(index, carry):
        cols = tile_of(index, wide)
        gain = gain_ref[:, cols].astype(f32)
        normed_ref[:, cols] = (mixed_ref[:, cols] * inverse * gain).astype(low)
        return carry

    lax.fori_loop(0, features // wide, normalize, 0)

    for step in order:
        w_copy(step).wait()

        def project(index, carry, step=step):
            rows = tile_of(index, tile, ahead[step] * block)
            value = lax.dot_general(
                normed_ref[...], w_ref[rows, :], dims(1, 1), preferred_element_type=f32
            )
            if step:
                part_mine[step, :, tile_of(index, tile)] = value.astype(low)
            else:
                own_part[:, tile_of(index, tile)] = value
            return carry

        lax.fori_loop(0, block // tile, project, 0)
        if step:
            part_copy(step).start()
    for step in range(1, groups):
        part_copy(step).wait()

    def finish(index, total):
        cols = tile_of(index, tile)
        projected = own_part[:, cols]
        for step in range(1, groups):
            projected = projected + part_land[step, :, cols].astype(f32)
        output_ref[:, cols] = projected.astype(low)
        grad = (projected - target_ref[:, cols].astype(f32)).astype(low)
        out_grad_ref[:, tile_of(index, tile, group * block)] = grad
        return total + jnp.sum(grad.astype(f32) * projected, axis=1, keepdims=True)

    product = lax.fori_loop(0, block // tile, finish, jnp.zeros((tok_count, 1), f32))
    product_mine[...] = jnp.broadcast_to(product, product_mine.shape)
    for step in range(1, groups):
        grad_copy(step, group).start()
        product_copy(step).start()

    def first_grad(index, carry):
        cols = tile_of(index, wide)
        rows = block_rows(group)
        normed_grad_ref[:, cols] = jnp.dot(
            out_grad_ref[:, rows], w_ref[rows, cols], preferred_element_type=f32
        )
        return carry

    lax.fori_loop(0, features // wide, first_grad, 0)
    for step in range(1, groups):
        grad_copy(step, group).wait_send()
        grad_copy(step, behind[step]).wait_recv()
        product_copy(step).wait()
        product = product + product_land[step][:, :1]
    inner = product / inverse
    pull = inverse**3 * inner / FEATURES

    def rest(index, carry):
        cols = tile_of(index, wide)
        grad = normed_grad_ref[:, cols]
        for step in range(1, groups):
            rows = block_rows(behind[step])
            grad = grad + jnp.dot(
                out_grad_ref[:, rows], w_ref[rows, cols], preferred_element_type=f32
            )
        mixed = mixed_ref[:, cols]
        gain = gain_ref[:, cols].astype(f32)
        gain_grad_ref[:, cols] = jnp.sum(grad * mixed * inverse, axis=0, keepdims=True)
        mixed_grad = (inverse * gain * grad - mixed * pull).astype(low)
        mixed_grad_ref[:, cols] = mixed_grad
        for half in range(wide // HEAD_DIM):
            head = index * (wide // HEAD_DIM) + half
            state = lax.dot_general(
                q_ref[:, columns_of(head)],
                mixed_grad[:, half * HEAD_DIM : (half + 1) * HEAD_DIM],
                dims(0, 0),
                preferred_element_type=f32,
            )
            state = state.reshape((per_head,) + mine_ref.shape[1:])
            mine_ref[pieces_of(head, per_head)] = state.astype(low)
        return carry

    lax.fori_loop(0, features // wide, rest, 0)
    exchange(count, me, mine_ref, spread_ref, first_send, first_recv)
    keep = causal(tok_count)

    def inside(head, carry):
        cols = columns_of(head)
        grad = mixed_grad_ref[:, cols]
        pairs = lax.dot_general(grad, v_ref[:, cols], dims(1, 1), preferred_element_type=f32)
        pairs = jnp.where(keep, pairs, 0.0).astype(low)
        state = state_ref[pieces_of(head, per_head)].reshape(HEAD_DIM, HEAD_DIM)
        query = jnp.dot(pairs, k_ref[:, cols], preferred_element_type=f32)
        query = query + lax.dot_general(grad, state, dims(1, 1), preferred_element_type=f32)
        query_ref[:, cols] = query.astype(low)
        key_part[:, cols] = lax.dot_general(
            pairs, q_ref[:, cols], dims(0, 0), preferred_element_type=f32
        )
        return carry

    def values(head, carry):
        cols = columns_of(head)
        normed_grad_ref[:, cols] = lax.dot_general(
            scores_ref[head], mixed_grad_ref[:, cols], dims(0, 0), preferred_element_type=f32
        )
        return carry

    lax.fori_loop(0, local_heads, inside, 0)
    exchange_wait(count, me, mine_ref, spread_ref, first_send, first_recv)
    running_sums(count, spread_ref, sums_ref, True)
    exchange(count, me, sums_ref, later_ref, second_send, second_recv)
    lax.fori_loop(0, local_heads, values, 0)
    exchange_wait(count, me, sums_ref, later_ref, second_send, second_recv)

    def last(head, carry):
        cols = columns_of(head)
        later = later_ref[pieces_of(head, per_head)].reshape(HEAD_DIM, HEAD_DIM)
        key = lax.dot_general(v_ref[:, cols], later, dims(1, 1), preferred_element_type=f32)
        key_ref[:, cols] = (key_part[:, cols] + key).astype(low)
        value = jnp.dot(k_ref[:, cols], later, preferred_element_type=f32)
        value_ref[:, cols] = (normed_grad_ref[:, cols] + value).astype(low)
        return carry

    lax.fori_loop(0, local_heads, last, 0)


def backward_part(mixed, gain, weight, target, queries, key_input, value_input, scores, state):
    count, groups = lax.axis_size("seq"), lax.axis_size("head")
    tok_count, features = queries.shape
    block = target.shape[1]
    width = weight.shape[0]
    low, f32 = jnp.bfloat16, jnp.float32
    vmem = pl.BlockSpec(memory_space=pltpu.VMEM)
    dma = pltpu.SemaphoreType.DMA
    flat = jax.ShapeDtypeStruct((tok_count, features), low)
    return pl.pallas_call(
        functools.partial(backward_kernel, count, groups),
        out_shape=(
            jax.ShapeDtypeStruct((tok_count, block), low),
            flat,
            jax.ShapeDtypeStruct((tok_count, width), low),
            flat,
            flat,
            flat,
            jax.ShapeDtypeStruct((1, features), f32),
        ),
        in_specs=[vmem, vmem, pl.BlockSpec(memory_space=pl.ANY)] + [vmem] * 6,
        out_specs=[vmem] * 7,
        scratch_shapes=[
            pltpu.VMEM((width, features), low),
            pltpu.VMEM((groups, tok_count, block), low),
            pltpu.VMEM((groups, tok_count, block), low),
            pltpu.VMEM((tok_count, block), f32),
            pltpu.VMEM((tok_count, 128), f32),
            pltpu.VMEM((groups, tok_count, 128), f32),
            pltpu.VMEM((tok_count, 128), f32),
            pltpu.VMEM((groups, tok_count, 128), f32),
            pltpu.VMEM((tok_count, features), f32),
            pltpu.VMEM((tok_count, features), f32),
            pltpu.VMEM((tok_count, features), low),
            pltpu.VMEM(state.shape, low),
            pltpu.VMEM(state.shape, low),
            pltpu.VMEM(state.shape, low),
            pltpu.VMEM(state.shape, low),
            dma((groups,)),
            dma((4, groups)),
            dma((4, groups)),
            dma((count,)),
            dma((count,)),
            dma((count,)),
            dma((count,)),
        ],
        compiler_params=pltpu.CompilerParams(collective_id=1, has_side_effects=True),
        name="backward_part",
    )(mixed, gain, weight, target, queries, key_input, value_input, scores, state)


def per_device(queries, key_input, value_input, norm_gain, out_weight, target):
    gathered, mixed, scores, state = forward_part(queries, key_input, value_input, out_weight.T)
    full_weight = gathered.reshape(-1, gathered.shape[2])
    output, normed, out_grad, query_grad, key_grad, value_grad, gain_grads = backward_part(
        mixed,
        norm_gain[None],
        full_weight,
        target,
        queries,
        key_input,
        value_input,
        scores,
        state,
    )
    weight_grads = lax.dot_general(
        normed, out_grad, (((0,), (0,)), ((), ())), preferred_element_type=jnp.float32
    ).astype(jnp.bfloat16)[None]
    return output, query_grad, key_grad, value_grad, gain_grads, weight_grads


def solution(mesh):
    placed = (
        P("seq", "head"),
        P("seq", "head"),
        P("seq", "head"),
        P("head"),
        P("head", "seq"),
        P("seq", "head"),
    )
    return jax.shard_map(
        per_device,
        mesh=mesh,
        in_specs=placed,
        out_specs=(
            P("seq", "head"),
            P("seq", "head"),
            P("seq", "head"),
            P("seq", "head"),
            P("seq", "head"),
            P("seq", "head", None),
        ),
        check_vma=False,
    )
```

```python
import functools

import jax
import jax.numpy as jnp
from jax import lax
from jax.experimental import pallas as pl
from jax.experimental.pallas import tpu as pltpu
from jax.sharding import PartitionSpec as P

HEAD_DIM = 128
FEATURES = 4096


EPSILON = 1e-06


def causal(count):
    row_index = lax.broadcasted_iota(jnp.int32, (count, count), 0)
    col_index = lax.broadcasted_iota(jnp.int32, (count, count), 1)
    return row_index >= col_index


def remote(src, dst, send_sem, recv_sem, peer, axis="seq"):
    return pltpu.make_async_remote_copy(
        src_ref=src,
        dst_ref=dst,
        send_sem=send_sem,
        recv_sem=recv_sem,
        device_id={axis: peer},
        device_id_type=pl.DeviceIdType.MESH,
    )


def exchange(count, me, source, target, send_sem, recv_sem):
    def start(step, carry):
        peer = lax.rem(me + step, count)
        remote(source.at[peer], target.at[me], send_sem.at[step], recv_sem.at[step], peer).start()
        return carry

    lax.fori_loop(1, count, start, 0)
    target[me] = source[me]


def exchange_wait(count, me, source, target, send_sem, recv_sem):
    def wait(step, carry):
        peer = lax.rem(me + step, count)
        origin = lax.rem(me - step + count, count)
        remote(source.at[peer], target.at[origin], send_sem.at[step], recv_sem.at[step], peer).wait()
        return carry

    lax.fori_loop(1, count, wait, 0)


def greet(*axes):
    barrier = pltpu.get_barrier_semaphore()
    for axis, count, me in axes:

        def signal(step, carry):
            pl.semaphore_signal(
                barrier,
                inc=1,
                device_id={axis: lax.rem(me + step, count)},
                device_id_type=pl.DeviceIdType.MESH,
            )
            return carry

        lax.fori_loop(1, count, signal, 0)
    pl.semaphore_wait(barrier, sum(count - 1 for _unused, count, _unused2 in axes))


def running_sums(count, source, target, backward):
    def one(step, total):
        index = count - 1 - step if backward else step
        target[index] = total.astype(jnp.bfloat16)
        return total + source[index].astype(jnp.float32)

    lax.fori_loop(0, count, one, jnp.zeros(source.shape[1:], jnp.float32))


def columns_of(head):
    return pl.ds(pl.multiple_of(head * HEAD_DIM, HEAD_DIM), HEAD_DIM)


def pieces_of(head, per_head):
    return pl.ds(head * per_head, per_head)


def dims(left, right):
    return (((left,), (right,)), ((), ()))


def forward_kernel(
    count,
    q_ref,
    k_ref,
    v_ref,
    w_ref,
    full_ref,
    mixed_ref,
    scores_ref,
    state_ref,
    mine_ref,
    spread_ref,
    sums_ref,
    x_sem,
    y_sem,
    up_sem,
    down_sem,
    land_sem,
    first_send,
    first_recv,
    second_send,
    second_recv,
    own_sem,
):
    f32 = jnp.float32
    me = lax.axis_index("seq")
    layers = count // 4
    layer, plane = me // 4, lax.rem(me, 4)
    row, col = plane // 2, lax.rem(plane, 2)
    plane_x = row * 2 + (1 - col)
    plane_y = (1 - row) * 2 + col
    plane_d = (1 - row) * 2 + (1 - col)
    x_peer = layer * 4 + plane_x
    y_peer = layer * 4 + plane_y
    features = w_ref.shape[1]
    blocks = features // 128
    cut_a = max(1, blocks * 3 // 16)
    cut_b = cut_a + (blocks - cut_a + 1) // 2
    edges = (0, cut_a * 128, cut_b * 128, features)
    piece = [pl.ds(edges[i], edges[i + 1] - edges[i]) for i in range(3)]
    local_heads = features // HEAD_DIM
    per_head = HEAD_DIM // mine_ref.shape[1]
    tok_count = q_ref.shape[0]

    def copy(shard, part, send_sem, peer, own=False):
        src = w_ref.at[:, piece[part]] if own else full_ref.at[shard, :, piece[part]]
        return remote(
            src, full_ref.at[shard, :, piece[part]], send_sem, land_sem.at[shard, part], peer
        )

    def landed(shard, part):
        copy(shard, part, x_sem.at[layers, 2], x_peer).wait_recv()

    def to_x(at, slot, shard, part, own=False):
        return copy(shard, part, x_sem.at[at, slot], x_peer, own)

    def to_y(at, slot, shard, part, own=False):
        return copy(shard, part, y_sem.at[at, slot], y_peer, own)

    def vertical(up, at, slot, shard, part, act, own=False, slack=None):
        sem, peer = (up_sem, me + 4) if up else (down_sem, me - 4)
        room = layers - 2 - layer if up else layer - 1
        room = room if slack is None else jnp.minimum(room, slack)

        @pl.when(room >= 0)
        def _():
            act(copy(shard, part, sem.at[at, slot], peer, own))

    def begin(transfer):
        transfer.start()

    def finish(transfer):
        transfer.wait_send()

    def own_sends(act):
        for part in (1, 2):
            for up in (True, False):
                vertical(up, layer, part - 1, me, part, act, True)
            act(to_x(layer, part - 1, me, part, True))
            act(to_y(layer, part - 1, me, part, True))
        act(to_x(layers, 0, me, 0, True))
        act(to_y(layers, 0, me, 0, True))
        for up in (True, False):
            vertical(up, layer, 2 + 0, me, 0, act, True)

    def sources(step):
        if step == 0:
            return ((layer, None, None),)
        return (
            (layer - step, layer - step, True),
            (layer + step, layers - 1 - layer - step, False),
        )

    def column_step(step, act, waiting):
        for at, slack, up in sources(step):
            shard = at * 4 + plane
            for part in (1, 2):

                @pl.when(slack >= 0)
                def _():
                    if waiting:
                        landed(shard, part)
                    act(to_x(at, part - 1, shard, part))
                    act(to_y(at, part - 1, shard, part))

                vertical(up, at, part - 1, shard, part, act, slack=slack)

    def guarded(slack, body):
        if slack is None:
            body()
        else:
            pl.when(slack >= 0)(body)

    def diagonal_step(step, act, waiting):
        for at, slack, _unused in sources(step):

            def body(at=at):
                if waiting:
                    landed(at * 4 + plane_y, 1)
                act(to_x(at, 2, at * 4 + plane_y, 1))
                if waiting:
                    landed(at * 4 + plane_x, 2)
                act(to_y(at, 2, at * 4 + plane_x, 2))

            guarded(slack, body)

    others = (plane_x, plane_y, plane_d)

    def plane_step(act, waiting):
        for slot, other in enumerate(others):
            shard = layer * 4 + other
            if waiting:
                landed(shard, 0)
            if slot == 0:
                act(to_y(layers, 1, shard, 0))
            for up in (True, False):
                vertical(up, layer, 3 + slot, shard, 0, act)

    def plane_chain(step, act, waiting):
        for at, slack, up in sources(step):
            for slot, other in enumerate((plane,) + others):
                shard = at * 4 + other
                if waiting:

                    @pl.when(slack >= 0)
                    def _():
                        landed(shard, 0)

                vertical(up, at, 2 + slot, shard, 0, act, slack=slack)

    greet(("seq", count, me))
    def outer(head, carry):
        cols = columns_of(head)
        state = lax.dot_general(
            k_ref[:, cols], v_ref[:, cols], dims(0, 0), preferred_element_type=f32
        )
        state = state.reshape((per_head,) + mine_ref.shape[1:])
        mine_ref[pieces_of(head, per_head)] = state.astype(jnp.bfloat16)
        return carry

    lax.fori_loop(0, local_heads, outer, 0)
    exchange(count, me, mine_ref, spread_ref, first_send, first_recv)
    own_sends(begin)
    own = pltpu.make_async_copy(w_ref, full_ref.at[me], own_sem)
    own.start()

    keep = causal(tok_count)

    def inside(head, carry):
        cols = columns_of(head)
        scores = lax.dot_general(
            q_ref[:, cols], k_ref[:, cols], dims(1, 1), preferred_element_type=f32
        )
        scores = jnp.where(keep, scores, 0.0).astype(jnp.bfloat16)
        scores_ref[head] = scores
        mixed_ref[:, cols] = jnp.dot(scores, v_ref[:, cols], preferred_element_type=f32)
        return carry

    lax.fori_loop(0, local_heads, inside, 0)
    exchange_wait(count, me, mine_ref, spread_ref, first_send, first_recv)
    running_sums(count, spread_ref, sums_ref, False)
    exchange(count, me, sums_ref, state_ref, second_send, second_recv)
    column_step(1, begin, True)
    diagonal_step(0, begin, True)
    plane_step(begin, True)
    for step in range(2, layers):
        column_step(step, begin, True)
        diagonal_step(step - 1, begin, True)
        plane_chain(step - 1, begin, True)
    diagonal_step(layers - 1, begin, True)
    plane_chain(layers - 1, begin, True)
    exchange_wait(count, me, sums_ref, state_ref, second_send, second_recv)

    def across(head, carry):
        cols = columns_of(head)
        state = state_ref[pieces_of(head, per_head)].reshape(HEAD_DIM, HEAD_DIM)
        mixed_ref[:, cols] += jnp.dot(q_ref[:, cols], state, preferred_element_type=f32)
        return carry

    lax.fori_loop(0, local_heads, across, 0)
    for at in range(layers):
        landed(at * 4 + plane_x, 1)
        landed(at * 4 + plane_y, 2)
        landed(at * 4 + plane_d, 1)
        landed(at * 4 + plane_d, 2)
    own_sends(finish)
    plane_step(finish, False)
    diagonal_step(0, finish, False)
    for step in range(1, layers):
        column_step(step, finish, False)
        diagonal_step(step, finish, False)
        plane_chain(step, finish, False)
    own.wait()


def forward_part(queries, key_input, value_input, weight):
    count = lax.axis_size("seq")
    tok_count, features = queries.shape
    local_heads = features // HEAD_DIM
    layers = count // 4
    piece_shape = (count, local_heads * HEAD_DIM // count, HEAD_DIM)
    low = jnp.bfloat16
    vmem = pl.BlockSpec(memory_space=pltpu.VMEM)
    dma = pltpu.SemaphoreType.DMA
    return pl.pallas_call(
        functools.partial(forward_kernel, count),
        out_shape=(
            jax.ShapeDtypeStruct((count,) + weight.shape, low),
            jax.ShapeDtypeStruct((tok_count, features), jnp.float32),
            jax.ShapeDtypeStruct((local_heads, tok_count, tok_count), low),
            jax.ShapeDtypeStruct(piece_shape, low),
        ),
        in_specs=[vmem] * 4,
        out_specs=(pl.BlockSpec(memory_space=pl.ANY), vmem, vmem, vmem),
        scratch_shapes=[
            pltpu.VMEM(piece_shape, low),
            pltpu.VMEM(piece_shape, low),
            pltpu.VMEM(piece_shape, low),
            dma((layers + 1, 3)),
            dma((layers + 1, 3)),
            dma((layers, 6)),
            dma((layers, 6)),
            dma((count, 3)),
            dma((count,)),
            dma((count,)),
            dma((count,)),
            dma((count,)),
            dma(()),
        ],
        compiler_params=pltpu.CompilerParams(collective_id=0, has_side_effects=True),
        name="forward_part",
    )(queries, key_input, value_input, weight)


def backward_kernel(
    count,
    groups,
    mixed_ref,
    gain_ref,
    w_hbm,
    target_ref,
    q_ref,
    k_ref,
    v_ref,
    scores_ref,
    state_ref,
    output_ref,
    normed_ref,
    out_grad_ref,
    query_ref,
    key_ref,
    value_ref,
    gain_grad_ref,
    w_ref,
    part_mine,
    part_land,
    own_part,
    square_mine,
    square_land,
    product_mine,
    product_land,
    normed_grad_ref,
    key_part,
    mixed_grad_ref,
    mine_ref,
    spread_ref,
    sums_ref,
    later_ref,
    w_sem,
    head_send,
    head_recv,
    first_send,
    first_recv,
    second_send,
    second_recv,
):
    f32 = jnp.float32
    low = jnp.bfloat16
    me = lax.axis_index("seq")
    group = lax.axis_index("head")
    tok_count, features = q_ref.shape
    block = target_ref.shape[1]
    tile = 256 if block % 256 == 0 else 128
    wide = 256
    local_heads = features // HEAD_DIM
    per_head = HEAD_DIM // mine_ref.shape[1]
    ahead = [lax.rem(group + step, groups) for step in range(groups)]
    behind = [lax.rem(group + groups - step, groups) for step in range(groups)]

    def block_rows(index):
        return pl.ds(pl.multiple_of(index * block, block), block)

    def tile_of(index, size, base=0):
        return pl.ds(pl.multiple_of(base + index * size, size), size)

    def w_copy(step):
        rows = block_rows(ahead[step])
        return pltpu.make_async_copy(w_hbm.at[rows], w_ref.at[rows], w_sem.at[step])

    def head_copy(kind, step, src, dst):
        return remote(
            src, dst, head_send.at[kind, step], head_recv.at[kind, step], ahead[step], "head"
        )

    def square_copy(step):
        return head_copy(0, step, square_mine, square_land.at[step])

    def part_copy(step):
        return head_copy(1, step, part_mine.at[step], part_land.at[step])

    def product_copy(step):
        return head_copy(2, step, product_mine, product_land.at[step])

    def grad_copy(step, index):
        cols = block_rows(index)
        return head_copy(3, step, out_grad_ref.at[:, cols], out_grad_ref.at[:, cols])

    order = list(range(1, groups)) + [0]
    for step in order:
        w_copy(step).start()
    greet(("seq", count, me), ("head", groups, group))

    def squared(index, total):
        value = mixed_ref[:, tile_of(index, wide)]
        return total + jnp.sum(value * value, axis=1, keepdims=True)

    squares = lax.fori_loop(0, features // wide, squared, jnp.zeros((tok_count, 1), f32))
    square_mine[...] = jnp.broadcast_to(squares, square_mine.shape)
    for step in range(1, groups):
        square_copy(step).start()
    for step in range(1, groups):
        square_copy(step).wait()
        squares = squares + square_land[step][:, :1]
    inverse = lax.rsqrt(squares / FEATURES + EPSILON)

    def normalize(index, carry):
        cols = tile_of(index, wide)
        gain = gain_ref[:, cols].astype(f32)
        normed_ref[:, cols] = (mixed_ref[:, cols] * inverse * gain).astype(low)
        return carry

    lax.fori_loop(0, features // wide, normalize, 0)

    for step in order:
        w_copy(step).wait()

        def project(index, carry, step=step):
            rows = tile_of(index, tile, ahead[step] * block)
            value = lax.dot_general(
                normed_ref[...], w_ref[rows, :], dims(1, 1), preferred_element_type=f32
            )
            if step:
                part_mine[step, :, tile_of(index, tile)] = value.astype(low)
            else:
                own_part[:, tile_of(index, tile)] = value
            return carry

        lax.fori_loop(0, block // tile, project, 0)
        if step:
            part_copy(step).start()
    for step in range(1, groups):
        part_copy(step).wait()

    def finish(index, total):
        cols = tile_of(index, tile)
        projected = own_part[:, cols]
        for step in range(1, groups):
            projected = projected + part_land[step, :, cols].astype(f32)
        output_ref[:, cols] = projected.astype(low)
        grad = (projected - target_ref[:, cols].astype(f32)).astype(low)
        out_grad_ref[:, tile_of(index, tile, group * block)] = grad
        return total + jnp.sum(grad.astype(f32) * projected, axis=1, keepdims=True)

    product = lax.fori_loop(0, block // tile, finish, jnp.zeros((tok_count, 1), f32))
    product_mine[...] = jnp.broadcast_to(product, product_mine.shape)
    for step in range(1, groups):
        grad_copy(step, group).start()
        product_copy(step).start()

    def first_grad(index, carry):
        cols = tile_of(index, wide)
        rows = block_rows(group)
        normed_grad_ref[:, cols] = jnp.dot(
            out_grad_ref[:, rows], w_ref[rows, cols], preferred_element_type=f32
        )
        return carry

    lax.fori_loop(0, features // wide, first_grad, 0)
    for step in range(1, groups):
        grad_copy(step, group).wait_send()
        grad_copy(step, behind[step]).wait_recv()
        product_copy(step).wait()
        product = product + product_land[step][:, :1]
    inner = product / inverse
    pull = inverse**3 * inner / FEATURES

    def rest(index, carry):
        cols = tile_of(index, wide)
        grad = normed_grad_ref[:, cols]
        for step in range(1, groups):
            rows = block_rows(behind[step])
            grad = grad + jnp.dot(
                out_grad_ref[:, rows], w_ref[rows, cols], preferred_element_type=f32
            )
        mixed = mixed_ref[:, cols]
        gain = gain_ref[:, cols].astype(f32)
        gain_grad_ref[:, cols] = jnp.sum(grad * mixed * inverse, axis=0, keepdims=True)
        mixed_grad = (inverse * gain * grad - mixed * pull).astype(low)
        mixed_grad_ref[:, cols] = mixed_grad
        for half in range(wide // HEAD_DIM):
            head = index * (wide // HEAD_DIM) + half
            state = lax.dot_general(
                q_ref[:, columns_of(head)],
                mixed_grad[:, half * HEAD_DIM : (half + 1) * HEAD_DIM],
                dims(0, 0),
                preferred_element_type=f32,
            )
            state = state.reshape((per_head,) + mine_ref.shape[1:])
            mine_ref[pieces_of(head, per_head)] = state.astype(low)
        return carry

    lax.fori_loop(0, features // wide, rest, 0)
    exchange(count, me, mine_ref, spread_ref, first_send, first_recv)
    keep = causal(tok_count)

    def inside(head, carry):
        cols = columns_of(head)
        grad = mixed_grad_ref[:, cols]
        pairs = lax.dot_general(grad, v_ref[:, cols], dims(1, 1), preferred_element_type=f32)
        pairs = jnp.where(keep, pairs, 0.0).astype(low)
        state = state_ref[pieces_of(head, per_head)].reshape(HEAD_DIM, HEAD_DIM)
        query = jnp.dot(pairs, k_ref[:, cols], preferred_element_type=f32)
        query = query + lax.dot_general(grad, state, dims(1, 1), preferred_element_type=f32)
        query_ref[:, cols] = query.astype(low)
        key_part[:, cols] = lax.dot_general(
            pairs, q_ref[:, cols], dims(0, 0), preferred_element_type=f32
        )
        return carry

    def values(head, carry):
        cols = columns_of(head)
        normed_grad_ref[:, cols] = lax.dot_general(
            scores_ref[head], mixed_grad_ref[:, cols], dims(0, 0), preferred_element_type=f32
        )
        return carry

    lax.fori_loop(0, local_heads, inside, 0)
    exchange_wait(count, me, mine_ref, spread_ref, first_send, first_recv)
    running_sums(count, spread_ref, sums_ref, True)
    exchange(count, me, sums_ref, later_ref, second_send, second_recv)
    lax.fori_loop(0, local_heads, values, 0)
    exchange_wait(count, me, sums_ref, later_ref, second_send, second_recv)

    def last(head, carry):
        cols = columns_of(head)
        later = later_ref[pieces_of(head, per_head)].reshape(HEAD_DIM, HEAD_DIM)
        key = lax.dot_general(v_ref[:, cols], later, dims(1, 1), preferred_element_type=f32)
        key_ref[:, cols] = (key_part[:, cols] + key).astype(low)
        value = jnp.dot(k_ref[:, cols], later, preferred_element_type=f32)
        value_ref[:, cols] = (normed_grad_ref[:, cols] + value).astype(low)
        return carry

    lax.fori_loop(0, local_heads, last, 0)


def backward_part(mixed, gain, weight, target, queries, key_input, value_input, scores, state):
    count, groups = lax.axis_size("seq"), lax.axis_size("head")
    tok_count, features = queries.shape
    block = target.shape[1]
    width = weight.shape[0]
    low, f32 = jnp.bfloat16, jnp.float32
    vmem = pl.BlockSpec(memory_space=pltpu.VMEM)
    dma = pltpu.SemaphoreType.DMA
    flat = jax.ShapeDtypeStruct((tok_count, features), low)
    return pl.pallas_call(
        functools.partial(backward_kernel, count, groups),
        out_shape=(
            jax.ShapeDtypeStruct((tok_count, block), low),
            flat,
            jax.ShapeDtypeStruct((tok_count, width), low),
            flat,
            flat,
            flat,
            jax.ShapeDtypeStruct((1, features), f32),
        ),
        in_specs=[vmem, vmem, pl.BlockSpec(memory_space=pl.ANY)] + [vmem] * 6,
        out_specs=[vmem] * 7,
        scratch_shapes=[
            pltpu.VMEM((width, features), low),
            pltpu.VMEM((groups, tok_count, block), low),
            pltpu.VMEM((groups, tok_count, block), low),
            pltpu.VMEM((tok_count, block), f32),
            pltpu.VMEM((tok_count, 128), f32),
            pltpu.VMEM((groups, tok_count, 128), f32),
            pltpu.VMEM((tok_count, 128), f32),
            pltpu.VMEM((groups, tok_count, 128), f32),
            pltpu.VMEM((tok_count, features), f32),
            pltpu.VMEM((tok_count, features), f32),
            pltpu.VMEM((tok_count, features), low),
            pltpu.VMEM(state.shape, low),
            pltpu.VMEM(state.shape, low),
            pltpu.VMEM(state.shape, low),
            pltpu.VMEM(state.shape, low),
            dma((groups,)),
            dma((4, groups)),
            dma((4, groups)),
            dma((count,)),
            dma((count,)),
            dma((count,)),
            dma((count,)),
        ],
        compiler_params=pltpu.CompilerParams(collective_id=1, has_side_effects=True),
        name="backward_part",
    )(mixed, gain, weight, target, queries, key_input, value_input, scores, state)


def per_device(queries, key_input, value_input, norm_gain, out_weight, target):
    gathered, mixed, scores, state = forward_part(queries, key_input, value_input, out_weight.T)
    full_weight = gathered.reshape(-1, gathered.shape[2])
    output, normed, out_grad, query_grad, key_grad, value_grad, gain_grads = backward_part(
        mixed,
        norm_gain[None],
        full_weight,
        target,
        queries,
        key_input,
        value_input,
        scores,
        state,
    )
    weight_grads = lax.dot_general(
        normed, out_grad, (((0,), (0,)), ((), ())), preferred_element_type=jnp.float32
    ).astype(jnp.bfloat16)[None]
    return output, query_grad, key_grad, value_grad, gain_grads, weight_grads


def solution(mesh):
    placed = (
        P("seq", "head"),
        P("seq", "head"),
        P("seq", "head"),
        P("head"),
        P("head", "seq"),
        P("seq", "head"),
    )
    return jax.shard_map(
        per_device,
        mesh=mesh,
        in_specs=placed,
        out_specs=(
            P("seq", "head"),
            P("seq", "head"),
            P("seq", "head"),
            P("seq", "head"),
            P("seq", "head"),
            P("seq", "head", None),
        ),
        check_vma=False,
    )
```

```python
import functools

import jax
import jax.numpy as jnp
from jax import lax
from jax.experimental import pallas as pl
from jax.experimental.pallas import tpu as pltpu
from jax.sharding import PartitionSpec as P

HEAD_DIM = 128
FEATURES = 4096


EPSILON = 1e-06


def causal(count):
    row_index = lax.broadcasted_iota(jnp.int32, (count, count), 0)
    col_index = lax.broadcasted_iota(jnp.int32, (count, count), 1)
    return row_index >= col_index


def remote(src, dst, send_sem, recv_sem, peer, axis="seq"):
    return pltpu.make_async_remote_copy(
        src_ref=src,
        dst_ref=dst,
        send_sem=send_sem,
        recv_sem=recv_sem,
        device_id={axis: peer},
        device_id_type=pl.DeviceIdType.MESH,
    )


def exchange(count, me, source, target, send_sem, recv_sem):
    def start(step, carry):
        peer = lax.rem(me + step, count)
        remote(source.at[peer], target.at[me], send_sem.at[step], recv_sem.at[step], peer).start()
        return carry

    lax.fori_loop(1, count, start, 0)
    target[me] = source[me]


def exchange_wait(count, me, source, target, send_sem, recv_sem):
    def wait(step, carry):
        peer = lax.rem(me + step, count)
        origin = lax.rem(me - step + count, count)
        remote(source.at[peer], target.at[origin], send_sem.at[step], recv_sem.at[step], peer).wait()
        return carry

    lax.fori_loop(1, count, wait, 0)


def greet(*axes):
    barrier = pltpu.get_barrier_semaphore()
    for axis, count, me in axes:

        def signal(step, carry):
            pl.semaphore_signal(
                barrier,
                inc=1,
                device_id={axis: lax.rem(me + step, count)},
                device_id_type=pl.DeviceIdType.MESH,
            )
            return carry

        lax.fori_loop(1, count, signal, 0)
    pl.semaphore_wait(barrier, sum(count - 1 for _unused, count, _unused2 in axes))


def running_sums(count, source, target, backward):
    def one(step, total):
        index = count - 1 - step if backward else step
        target[index] = total.astype(jnp.bfloat16)
        return total + source[index].astype(jnp.float32)

    lax.fori_loop(0, count, one, jnp.zeros(source.shape[1:], jnp.float32))


def columns_of(head):
    return pl.ds(pl.multiple_of(head * HEAD_DIM, HEAD_DIM), HEAD_DIM)


def pieces_of(head, per_head):
    return pl.ds(head * per_head, per_head)


def dims(left, right):
    return (((left,), (right,)), ((), ()))


def kernel(
    count,
    groups,
    q_ref,
    k_ref,
    v_ref,
    w_ref,
    gain_ref,
    target_ref,
    output_ref,
    normed_ref,
    out_grad_ref,
    query_ref,
    key_ref,
    value_ref,
    gain_grad_ref,
    full_ref,
    mixed_ref,
    scores_ref,
    state_ref,
    mine_ref,
    spread_ref,
    sums_ref,
    later_mine_ref,
    later_spread_ref,
    later_sums_ref,
    later_ref,
    part_mine,
    part_land,
    own_part,
    square_mine,
    square_land,
    product_mine,
    product_land,
    normed_grad_ref,
    key_part,
    mixed_grad_ref,
    x_sem,
    y_sem,
    up_sem,
    down_sem,
    land_sem,
    own_sem,
    head_send,
    head_recv,
    first_send,
    first_recv,
    second_send,
    second_recv,
    back_first_send,
    back_first_recv,
    back_second_send,
    back_second_recv,
):
    f32 = jnp.float32
    low = jnp.bfloat16
    me = lax.axis_index("seq")
    group = lax.axis_index("head")
    layers = count // 4
    layer, plane = me // 4, lax.rem(me, 4)
    row, col = plane // 2, lax.rem(plane, 2)
    plane_x = row * 2 + (1 - col)
    plane_y = (1 - row) * 2 + col
    plane_d = (1 - row) * 2 + (1 - col)
    x_peer = layer * 4 + plane_x
    y_peer = layer * 4 + plane_y
    features = w_ref.shape[1]
    blocks = features // 128
    cut_a = max(1, blocks * 3 // 16)
    cut_b = cut_a + (blocks - cut_a + 1) // 2
    edges = (0, cut_a * 128, cut_b * 128, features)
    piece = [pl.ds(edges[i], edges[i + 1] - edges[i]) for i in range(3)]
    local_heads = features // HEAD_DIM
    per_head = HEAD_DIM // mine_ref.shape[1]
    tok_count = q_ref.shape[0]

    share = w_ref.shape[0]

    def shard_rows(shard):
        return pl.ds(pl.multiple_of(shard * share, share), share)

    def copy(shard, part, send_sem, peer, own=False):
        target = full_ref.at[shard_rows(shard), piece[part]]
        src = w_ref.at[:, piece[part]] if own else target
        return remote(src, target, send_sem, land_sem.at[shard, part], peer)

    def landed(shard, part):
        copy(shard, part, x_sem.at[layers, 2], x_peer).wait_recv()

    def to_x(at, slot, shard, part, own=False):
        return copy(shard, part, x_sem.at[at, slot], x_peer, own)

    def to_y(at, slot, shard, part, own=False):
        return copy(shard, part, y_sem.at[at, slot], y_peer, own)

    def vertical(up, at, slot, shard, part, act, own=False, slack=None):
        sem, peer = (up_sem, me + 4) if up else (down_sem, me - 4)
        room = layers - 2 - layer if up else layer - 1
        room = room if slack is None else jnp.minimum(room, slack)

        @pl.when(room >= 0)
        def _():
            act(copy(shard, part, sem.at[at, slot], peer, own))

    def begin(transfer):
        transfer.start()

    def finish(transfer):
        transfer.wait_send()

    def own_sends(act):
        for part in (1, 2):
            for up in (True, False):
                vertical(up, layer, part - 1, me, part, act, True)
            act(to_x(layer, part - 1, me, part, True))
            act(to_y(layer, part - 1, me, part, True))
        act(to_x(layers, 0, me, 0, True))
        act(to_y(layers, 0, me, 0, True))
        for up in (True, False):
            vertical(up, layer, 2 + 0, me, 0, act, True)

    def sources(step):
        if step == 0:
            return ((layer, None, None),)
        return (
            (layer - step, layer - step, True),
            (layer + step, layers - 1 - layer - step, False),
        )

    def column_step(step, act, waiting):
        for at, slack, up in sources(step):
            shard = at * 4 + plane
            for part in (1, 2):

                @pl.when(slack >= 0)
                def _():
                    if waiting:
                        landed(shard, part)
                    act(to_x(at, part - 1, shard, part))
                    act(to_y(at, part - 1, shard, part))

                vertical(up, at, part - 1, shard, part, act, slack=slack)

    def guarded(slack, body):
        if slack is None:
            body()
        else:
            pl.when(slack >= 0)(body)

    def diagonal_step(step, act, waiting):
        for at, slack, _unused in sources(step):

            def body(at=at):
                if waiting:
                    landed(at * 4 + plane_y, 1)
                act(to_x(at, 2, at * 4 + plane_y, 1))
                if waiting:
                    landed(at * 4 + plane_x, 2)
                act(to_y(at, 2, at * 4 + plane_x, 2))

            guarded(slack, body)

    others = (plane_x, plane_y, plane_d)

    def plane_step(act, waiting):
        for slot, other in enumerate(others):
            shard = layer * 4 + other
            if waiting:
                landed(shard, 0)
            if slot == 0:
                act(to_y(layers, 1, shard, 0))
            for up in (True, False):
                vertical(up, layer, 3 + slot, shard, 0, act)

    def plane_chain(step, act, waiting):
        for at, slack, up in sources(step):
            for slot, other in enumerate((plane,) + others):
                shard = at * 4 + other
                if waiting:

                    @pl.when(slack >= 0)
                    def _():
                        landed(shard, 0)

                vertical(up, at, 2 + slot, shard, 0, act, slack=slack)

    greet(("seq", count, me), ("head", groups, group))
    def outer(head, carry):
        cols = columns_of(head)
        state = lax.dot_general(
            k_ref[:, cols], v_ref[:, cols], dims(0, 0), preferred_element_type=f32
        )
        state = state.reshape((per_head,) + mine_ref.shape[1:])
        mine_ref[pieces_of(head, per_head)] = state.astype(jnp.bfloat16)
        return carry

    lax.fori_loop(0, local_heads, outer, 0)
    exchange(count, me, mine_ref, spread_ref, first_send, first_recv)
    own_sends(begin)
    own = pltpu.make_async_copy(w_ref, full_ref.at[shard_rows(me)], own_sem)
    own.start()

    keep = causal(tok_count)

    def inside(head, carry):
        cols = columns_of(head)
        scores = lax.dot_general(
            q_ref[:, cols], k_ref[:, cols], dims(1, 1), preferred_element_type=f32
        )
        scores = jnp.where(keep, scores, 0.0).astype(jnp.bfloat16)
        scores_ref[head] = scores
        mixed_ref[:, cols] = jnp.dot(scores, v_ref[:, cols], preferred_element_type=f32)
        return carry

    lax.fori_loop(0, local_heads, inside, 0)
    exchange_wait(count, me, mine_ref, spread_ref, first_send, first_recv)
    running_sums(count, spread_ref, sums_ref, False)
    exchange(count, me, sums_ref, state_ref, second_send, second_recv)
    column_step(1, begin, True)
    diagonal_step(0, begin, True)
    plane_step(begin, True)
    for step in range(2, layers):
        column_step(step, begin, True)
        diagonal_step(step - 1, begin, True)
        plane_chain(step - 1, begin, True)
    diagonal_step(layers - 1, begin, True)
    plane_chain(layers - 1, begin, True)
    exchange_wait(count, me, sums_ref, state_ref, second_send, second_recv)

    def across(head, carry):
        cols = columns_of(head)
        state = state_ref[pieces_of(head, per_head)].reshape(HEAD_DIM, HEAD_DIM)
        mixed_ref[:, cols] += jnp.dot(q_ref[:, cols], state, preferred_element_type=f32)
        return carry

    lax.fori_loop(0, local_heads, across, 0)
    block = target_ref.shape[1]
    tile = 256 if block % 256 == 0 else 128
    wide = 256
    ahead = [lax.rem(group + step, groups) for step in range(groups)]
    behind = [lax.rem(group + groups - step, groups) for step in range(groups)]

    def block_rows(index):
        return pl.ds(pl.multiple_of(index * block, block), block)

    def tile_of(index, size, base=0):
        return pl.ds(pl.multiple_of(base + index * size, size), size)

    def head_copy(kind, step, src, dst):
        return remote(
            src, dst, head_send.at[kind, step], head_recv.at[kind, step], ahead[step], "head"
        )

    def square_copy(step):
        return head_copy(0, step, square_mine, square_land.at[step])

    def part_copy(step):
        return head_copy(1, step, part_mine.at[step], part_land.at[step])

    def product_copy(step):
        return head_copy(2, step, product_mine, product_land.at[step])

    def grad_copy(step, index):
        cols = block_rows(index)
        return head_copy(3, step, out_grad_ref.at[:, cols], out_grad_ref.at[:, cols])

    order = list(range(1, groups)) + [0]

    def squared(index, total):
        value = mixed_ref[:, tile_of(index, wide)]
        return total + jnp.sum(value * value, axis=1, keepdims=True)

    squares = lax.fori_loop(0, features // wide, squared, jnp.zeros((tok_count, 1), f32))
    square_mine[...] = jnp.broadcast_to(squares, square_mine.shape)
    for step in range(1, groups):
        square_copy(step).start()
    for step in range(1, groups):
        square_copy(step).wait()
        squares = squares + square_land[step][:, :1]
    inverse = lax.rsqrt(squares / FEATURES + EPSILON)

    def normalize(index, carry):
        cols = tile_of(index, wide)
        gain = gain_ref[:, cols].astype(f32)
        normed_ref[:, cols] = (mixed_ref[:, cols] * inverse * gain).astype(low)
        return carry

    lax.fori_loop(0, features // wide, normalize, 0)

    for at in range(layers):
        landed(at * 4 + plane_x, 1)
        landed(at * 4 + plane_y, 2)
        landed(at * 4 + plane_d, 1)
        landed(at * 4 + plane_d, 2)
    own.wait()
    for step in order:

        def project(index, carry, step=step):
            rows = tile_of(index, tile, ahead[step] * block)
            value = lax.dot_general(
                normed_ref[...], full_ref[rows, :], dims(1, 1), preferred_element_type=f32
            )
            if step:
                part_mine[step, :, tile_of(index, tile)] = value.astype(low)
            else:
                own_part[:, tile_of(index, tile)] = value
            return carry

        lax.fori_loop(0, block // tile, project, 0)
        if step:
            part_copy(step).start()
    for step in range(1, groups):
        part_copy(step).wait()

    def settle(index, total):
        cols = tile_of(index, tile)
        projected = own_part[:, cols]
        for step in range(1, groups):
            projected = projected + part_land[step, :, cols].astype(f32)
        output_ref[:, cols] = projected.astype(low)
        grad = (projected - target_ref[:, cols].astype(f32)).astype(low)
        out_grad_ref[:, tile_of(index, tile, group * block)] = grad
        return total + jnp.sum(grad.astype(f32) * projected, axis=1, keepdims=True)

    product = lax.fori_loop(0, block // tile, settle, jnp.zeros((tok_count, 1), f32))
    product_mine[...] = jnp.broadcast_to(product, product_mine.shape)
    for step in range(1, groups):
        grad_copy(step, group).start()
        product_copy(step).start()

    def first_grad(index, carry):
        cols = tile_of(index, wide)
        rows = block_rows(group)
        normed_grad_ref[:, cols] = jnp.dot(
            out_grad_ref[:, rows], full_ref[rows, cols], preferred_element_type=f32
        )
        return carry

    lax.fori_loop(0, features // wide, first_grad, 0)
    for step in range(1, groups):
        grad_copy(step, group).wait_send()
        grad_copy(step, behind[step]).wait_recv()
        product_copy(step).wait()
        product = product + product_land[step][:, :1]
    inner = product / inverse
    pull = inverse**3 * inner / FEATURES

    def rest(index, carry):
        cols = tile_of(index, wide)
        grad = normed_grad_ref[:, cols]
        for step in range(1, groups):
            rows = block_rows(behind[step])
            grad = grad + jnp.dot(
                out_grad_ref[:, rows], full_ref[rows, cols], preferred_element_type=f32
            )
        mixed = mixed_ref[:, cols]
        gain = gain_ref[:, cols].astype(f32)
        gain_grad_ref[:, cols] = jnp.sum(grad * mixed * inverse, axis=0, keepdims=True)
        mixed_grad = (inverse * gain * grad - mixed * pull).astype(low)
        mixed_grad_ref[:, cols] = mixed_grad
        for half in range(wide // HEAD_DIM):
            head = index * (wide // HEAD_DIM) + half
            state = lax.dot_general(
                q_ref[:, columns_of(head)],
                mixed_grad[:, half * HEAD_DIM : (half + 1) * HEAD_DIM],
                dims(0, 0),
                preferred_element_type=f32,
            )
            state = state.reshape((per_head,) + later_mine_ref.shape[1:])
            later_mine_ref[pieces_of(head, per_head)] = state.astype(low)
        return carry

    lax.fori_loop(0, features // wide, rest, 0)
    exchange(count, me, later_mine_ref, later_spread_ref, back_first_send, back_first_recv)

    def paired(head, carry):
        cols = columns_of(head)
        grad = mixed_grad_ref[:, cols]
        pairs = lax.dot_general(grad, v_ref[:, cols], dims(1, 1), preferred_element_type=f32)
        pairs = jnp.where(keep, pairs, 0.0).astype(low)
        state = state_ref[pieces_of(head, per_head)].reshape(HEAD_DIM, HEAD_DIM)
        query = jnp.dot(pairs, k_ref[:, cols], preferred_element_type=f32)
        query = query + lax.dot_general(grad, state, dims(1, 1), preferred_element_type=f32)
        query_ref[:, cols] = query.astype(low)
        key_part[:, cols] = lax.dot_general(
            pairs, q_ref[:, cols], dims(0, 0), preferred_element_type=f32
        )
        return carry

    def values(head, carry):
        cols = columns_of(head)
        normed_grad_ref[:, cols] = lax.dot_general(
            scores_ref[head], mixed_grad_ref[:, cols], dims(0, 0), preferred_element_type=f32
        )
        return carry

    lax.fori_loop(0, local_heads, paired, 0)
    exchange_wait(count, me, later_mine_ref, later_spread_ref, back_first_send, back_first_recv)
    running_sums(count, later_spread_ref, later_sums_ref, True)
    exchange(count, me, later_sums_ref, later_ref, back_second_send, back_second_recv)
    lax.fori_loop(0, local_heads, values, 0)
    exchange_wait(count, me, later_sums_ref, later_ref, back_second_send, back_second_recv)

    def last(head, carry):
        cols = columns_of(head)
        later = later_ref[pieces_of(head, per_head)].reshape(HEAD_DIM, HEAD_DIM)
        key = lax.dot_general(v_ref[:, cols], later, dims(1, 1), preferred_element_type=f32)
        key_ref[:, cols] = (key_part[:, cols] + key).astype(low)
        value = jnp.dot(k_ref[:, cols], later, preferred_element_type=f32)
        value_ref[:, cols] = (normed_grad_ref[:, cols] + value).astype(low)
        return carry

    lax.fori_loop(0, local_heads, last, 0)
    own_sends(finish)
    plane_step(finish, False)
    diagonal_step(0, finish, False)
    for step in range(1, layers):
        column_step(step, finish, False)
        diagonal_step(step, finish, False)
        plane_chain(step, finish, False)


def fused(queries, key_input, value_input, weight, gain, target):
    count, groups = lax.axis_size("seq"), lax.axis_size("head")
    tok_count, features = queries.shape
    local_heads = features // HEAD_DIM
    layers = count // 4
    block = target.shape[1]
    width = count * weight.shape[0]
    low, f32 = jnp.bfloat16, jnp.float32
    pieces = pltpu.VMEM((count, local_heads * HEAD_DIM // count, HEAD_DIM), low)
    flat = jax.ShapeDtypeStruct((tok_count, features), low)
    vmem = pl.BlockSpec(memory_space=pltpu.VMEM)
    dma = pltpu.SemaphoreType.DMA
    return pl.pallas_call(
        functools.partial(kernel, count, groups),
        out_shape=(
            jax.ShapeDtypeStruct((tok_count, block), low),
            flat,
            jax.ShapeDtypeStruct((tok_count, width), low),
            flat,
            flat,
            flat,
            jax.ShapeDtypeStruct((1, features), f32),
        ),
        in_specs=[vmem] * 6,
        out_specs=[vmem] * 7,
        scratch_shapes=[
            pltpu.VMEM((width, features), low),
            pltpu.VMEM((tok_count, features), f32),
            pltpu.VMEM((local_heads, tok_count, tok_count), low),
        ]
        + [pieces] * 8
        + [
            pltpu.VMEM((groups, tok_count, block), low),
            pltpu.VMEM((groups, tok_count, block), low),
            pltpu.VMEM((tok_count, block), f32),
            pltpu.VMEM((tok_count, 128), f32),
            pltpu.VMEM((groups, tok_count, 128), f32),
            pltpu.VMEM((tok_count, 128), f32),
            pltpu.VMEM((groups, tok_count, 128), f32),
            pltpu.VMEM((tok_count, features), f32),
            pltpu.VMEM((tok_count, features), f32),
            pltpu.VMEM((tok_count, features), low),
            dma((layers + 1, 3)),
            dma((layers + 1, 3)),
            dma((layers, 6)),
            dma((layers, 6)),
            dma((count, 3)),
            dma(()),
            dma((4, groups)),
            dma((4, groups)),
        ]
        + [dma((count,))] * 8,
        compiler_params=pltpu.CompilerParams(collective_id=0, has_side_effects=True),
        name="fused",
    )(queries, key_input, value_input, weight, gain, target)


def per_device(queries, key_input, value_input, norm_gain, out_weight, target):
    output, normed, out_grad, query_grad, key_grad, value_grad, gain_grads = fused(
        queries, key_input, value_input, out_weight.T, norm_gain[None], target
    )
    weight_grads = lax.dot_general(
        normed, out_grad, (((0,), (0,)), ((), ())), preferred_element_type=jnp.float32
    ).astype(jnp.bfloat16)[None]
    return output, query_grad, key_grad, value_grad, gain_grads, weight_grads


def solution(mesh):
    placed = (
        P("seq", "head"),
        P("seq", "head"),
        P("seq", "head"),
        P("head"),
        P("head", "seq"),
        P("seq", "head"),
    )
    return jax.shard_map(
        per_device,
        mesh=mesh,
        in_specs=placed,
        out_specs=(
            P("seq", "head"),
            P("seq", "head"),
            P("seq", "head"),
            P("seq", "head"),
            P("seq", "head"),
            P("seq", "head", None),
        ),
        check_vma=False,
    )
```
